32 devices in a mesh: feat: 8 (over z, y), tok: 4 (over x, core).
Axes of the slice: x: 2, y: 2, z: 4, core: 2. Of those that a mesh axis runs over, the one named last changes fastest.
Arguments:
- tokens: bfloat16 [4096, 8192], P('tok', 'feat'), parts along dimension 0, may hold values from -6 to 6
- pair_weights: bfloat16 [2, 2048, 8192], P(None, None, 'feat'), may hold values from -0.125 to 0.125
- rank_down: bfloat16 [8192, 256], P('feat'), may hold values from -0.0625 to 0.0625
- rank_up: bfloat16 [256, 8192], P(None, 'feat'), may hold values from -0.375 to 0.375
Outputs:
- mixed: bfloat16 [4096, 8192], P('tok', 'feat'), parts along dimension 0
The draws below stay inside these ranges and needn't reach their ends.
There are 4 independent parts, one for each index of `tok`. The reference program is written for one: setup_inputs(seed, part) draws one part's arguments, and reference() takes and returns one part's arrays. A program takes and returns all parts, laid end to end along the dimension named above; an argument that names none is the same for every part. Nothing has to cross between parts.
All inputs are finite; a program needn't handle non-finite values.
Results may differ from the reference program's by a relative error of at most 0.0049.
Values may be sent and summed in bfloat16 or wider, within the bound.
A program may use at most 64 MiB of HBM per device.

```python
import jax
import jax.numpy as jnp
import numpy as np

BLOCK = 1024
RANK = 256
SECTIONS = 2
TOK = 1024
D = 8192
N_FEAT = 8


def block_levels(stream_key, shape, shards, smallest, largest):
    def one(position, blocks):
        heights = jax.random.uniform(jax.random.fold_in(jax.random.fold_in(stream_key, 6), position), (blocks,), jnp.float32, smallest / len(shards), largest / len(shards))
        return jnp.repeat(jnp.exp(heights), shape[position] // blocks).reshape((-1,) + (1,) * (len(shape) - position - 1))

    gain = one(*shards[0])
    for cut in shards[1:]:
        gain = gain * one(*cut)
    return gain


def gaussian(stream_key, shape, spread, bound, cuts=(), kind=jnp.bfloat16):
    values = jax.random.normal(stream_key, shape, jnp.float32) * spread
    if len(cuts) > 0:
        values = block_levels(stream_key, shape, cuts, -0.22, 0.18) * values
    return jnp.clip(values, min=-bound, max=bound).astype(kind)


def setup_inputs(seed: int = 0, part: int = 0) -> dict:
    seeds = jax.random.split(jax.random.key(seed), 5)
    own_keys = jax.random.split(jax.random.fold_in(seeds[4], part), 5)
    return {
        "tokens": gaussian(own_keys[0], (TOK, D), 1.0, 6.0, ((1, 8),)),
        "pair_weights": gaussian(seeds[1], (SECTIONS, 2 * BLOCK, D), (2 * BLOCK) ** -0.5, 0.125, ((2, 8),)),
        "rank_down": gaussian(seeds[2], (D, RANK), D ** -0.5, 0.0625, ((0, 8),)),
        "rank_up": gaussian(seeds[3], (RANK, D), RANK ** -0.5, 0.375, ((1, 8),)),
    }


def section_apply(current, section_weight, bit_number):
    blocked = current.reshape(TOK, N_FEAT, BLOCK).astype(jnp.float32)
    order = np.arange(N_FEAT) ^ (1 << bit_number)
    partner_blocks = blocked[:, order, :]
    weight_blocks = section_weight.reshape(2 * BLOCK, N_FEAT, BLOCK).astype(jnp.float32)
    own_part = jnp.einsum("tkb,bkc->tkc", blocked, weight_blocks[:BLOCK])
    other_part = jnp.einsum("tkb,bkc->tkc", partner_blocks, weight_blocks[BLOCK:])
    return (own_part + other_part).reshape(TOK, N_FEAT * BLOCK)


def reference(tokens, pair_weights, rank_down, rank_up):
    bit_levels = N_FEAT.bit_length() - 1
    current = tokens
    activated = None
    for section_index in range(SECTIONS):
        bit_number = section_index * (bit_levels - 1) // (SECTIONS - 1)
        pre_act = section_apply(current, pair_weights[section_index], bit_number)
        activated = jax.nn.silu(pre_act)
        current = activated.astype(jnp.bfloat16)
    low_rank = jnp.dot(tokens, rank_down, preferred_element_type=jnp.float32).astype(jnp.bfloat16)
    branch_out = jnp.dot(low_rank, rank_up, preferred_element_type=jnp.float32)
    return (activated + branch_out).astype(jnp.bfloat16)
```

```python
import functools

import jax
import jax.numpy as jnp
from jax import lax
from jax.experimental import pallas as pl
from jax.experimental.pallas import tpu as pltpu
from jax.sharding import PartitionSpec as P

CHUNKS = 8
MESH = pl.DeviceIdType.MESH


def silu(v):
    return v / (1.0 + jnp.exp(-v))


def flip(me, bits):
    other = me
    for b in bits:
        other = other + (1 - 2 * ((me // (1 << b)) % 2)) * (1 << b)
    return other


def kernel(
    levels, x_hbm, w_hbm, down_hbm, up_hbm, out_hbm,
    x, w0, w1, down, up, xp, state, sp, out,
    acc, low, send_buf, recv_buf, end_recv, mid_recv, end_send, mid_send,
    load_sem, out_sem, ys, yr, zs, zr, rs_s, rs_r, ag_s, ag_r,
    end_s, end_r, mid_s, mid_r, back_s, back_r,
):
    me = lax.axis_index("feat")
    tok, width = x.shape
    rows = tok // CHUNKS
    top = levels - 1
    inner = top - 1

    loads = [
        pltpu.make_async_copy(src, dst, load_sem.at[i])
        for i, (src, dst) in enumerate(
            ((x_hbm, x), (down_hbm, down), (w_hbm.at[0], w0), (w_hbm.at[1], w1), (up_hbm, up))
        )
    ]
    for load in loads:
        load.start()

    partners = [flip(me, (b,)) for b in range(levels)] + [flip(me, (inner, top))]
    barrier = pltpu.get_barrier_semaphore()
    for other in partners:
        pl.semaphore_signal(barrier, inc=1, device_id={"feat": other}, device_id_type=MESH)
    pl.semaphore_wait(barrier, len(partners))

    def remote(src, dst, send, recv, other):
        return pltpu.make_async_remote_copy(
            src_ref=src, dst_ref=dst, send_sem=send, recv_sem=recv,
            device_id={"feat": other}, device_id_type=MESH,
        )

    def part(c):
        return pl.ds(pl.multiple_of(c * rows, rows), rows)

    def y_copy(c):
        return remote(x_hbm.at[part(c)], xp.at[part(c)], ys.at[c], yr.at[c], partners[0])

    def z_copy(c):
        return remote(state.at[part(c)], sp.at[part(c)], zs.at[c], zr.at[c], partners[top])

    def out_copy(c):
        return pltpu.make_async_copy(out.at[part(c)], out_hbm.at[part(c)], out_sem.at[c])

    y_copy(0).start()

    loads[0].wait()
    loads[1].wait()
    bit = [(me // (1 << b)) % 2 for b in range(levels)]
    step_rows = tok // 8

    def project(offset, count):
        @pl.loop(0, count // step_rows)
        def _(i):
            span = pl.ds(pl.multiple_of(offset + i * step_rows, step_rows), step_rows)
            acc[span, :] = jnp.dot(x[span, :], down[...], preferred_element_type=jnp.float32)

    def span_of(offset, count):
        return pl.ds(pl.multiple_of(offset, count), count)

    half = tok // 2
    keep = bit[0] * half
    away = (1 - bit[0]) * half
    project(away, half)
    spans = [(keep, away, half)]
    for b in range(1, inner):
        size = spans[-1][2] // 2
        base = spans[-1][0]
        spans.append((base + bit[b] * size, base + (1 - bit[b]) * size, size))

    def rs_copy(b):
        size = spans[b][2]
        start = tok - 2 * size
        return remote(
            send_buf.at[pl.ds(start, size)], recv_buf.at[pl.ds(start, size)],
            rs_s.at[b], rs_r.at[b], partners[b],
        )

    def rs_start(b):
        _, gone, size = spans[b]
        send_buf[pl.ds(tok - 2 * size, size), :] = acc[span_of(gone, size), :].astype(jnp.bfloat16)
        rs_copy(b).start()

    def rs_finish(b):
        kept, _, size = spans[b]
        rs_copy(b).wait_recv()
        acc[span_of(kept, size), :] += recv_buf[pl.ds(tok - 2 * size, size), :].astype(jnp.float32)

    rs_start(0)
    for c in range(1, CHUNKS):
        y_copy(c).start()
    project(keep, half)

    own, _, own_size = spans[-1]
    own_span = span_of(own, own_size)
    middle = (bit[inner] + bit[top]) % 2
    end_copy = remote(end_send, end_recv, end_s.at[0], end_r.at[0], partners[inner])
    mid_copy = remote(mid_send, mid_recv, mid_s.at[0], mid_r.at[0], partners[levels])
    back_copy = remote(low.at[own_span], low.at[own_span], back_s.at[0], back_r.at[0], partners[inner])

    def to_middle():
        @pl.when(middle == 0)
        def _():
            end_send[...] = acc[own_span, :].astype(jnp.bfloat16)
            end_copy.start()

    def across():
        @pl.when(middle == 1)
        def _():
            end_copy.wait_recv()
            acc[own_span, :] += end_recv[...].astype(jnp.float32)
            mid_send[...] = acc[own_span, :].astype(jnp.bfloat16)
            mid_copy.start()

    def back():
        @pl.when(middle == 1)
        def _():
            mid_copy.wait_recv()
            low[own_span, :] = (acc[own_span, :] + mid_recv[...].astype(jnp.float32)).astype(jnp.bfloat16)
            back_copy.start()

    def ag_copy(b):
        size = tok >> (b + 1)
        span = span_of(spans[b][0], size)
        return remote(low.at[span], low.at[span], ag_s.at[b], ag_r.at[b], partners[b])

    columns = 512
    column_tiles = width // columns

    def first_section(c):
        y_copy(c).wait_recv()

        @pl.loop(0, column_tiles)
        def _(t):
            cols = pl.ds(pl.multiple_of(t * columns, columns), columns)
            pre = jnp.dot(x[part(c), :], w0[:width, cols], preferred_element_type=jnp.float32)
            pre += jnp.dot(xp[part(c), :], w0[width:, cols], preferred_element_type=jnp.float32)
            state[part(c), cols] = silu(pre).astype(jnp.bfloat16)

        z_copy(c).start()

    def second_section(c):
        z_copy(c).wait_recv()

        @pl.loop(0, column_tiles)
        def _(t):
            cols = pl.ds(pl.multiple_of(t * columns, columns), columns)
            pre = jnp.dot(state[part(c), :], w1[:width, cols], preferred_element_type=jnp.float32)
            pre += jnp.dot(sp[part(c), :], w1[width:, cols], preferred_element_type=jnp.float32)
            side = jnp.dot(low[part(c), :], up[:, cols], preferred_element_type=jnp.float32)
            out[part(c), cols] = (silu(pre) + side).astype(jnp.bfloat16)

        out_copy(c).start()

    loads[2].wait()
    first_section(0)
    for b in range(inner):
        rs_finish(b)
        if b + 1 < inner:
            rs_start(b + 1)
    to_middle()

    @pl.loop(1, 3)
    def _(c):
        first_section(c)

    across()

    @pl.loop(3, CHUNKS)
    def _(c):
        first_section(c)

    back()

    @pl.when(middle == 0)
    def _():
        back_copy.wait_recv()

    for b in range(inner - 1, -1, -1):
        ag_copy(b).start()
        ag_copy(b).wait_recv()

    loads[3].wait()
    loads[4].wait()

    @pl.loop(0, CHUNKS)
    def _(c):
        second_section(c)

    @pl.loop(0, CHUNKS)
    def _(c):
        y_copy(c).wait_send()
        z_copy(c).wait_send()
        out_copy(c).wait()

    for b in range(inner):
        rs_copy(b).wait_send()
        ag_copy(b).wait_send()

    @pl.when(middle == 0)
    def _():
        end_copy.wait_send()

    @pl.when(middle == 1)
    def _():
        mid_copy.wait_send()
        back_copy.wait_send()


def on_device(tokens, pair_weights, rank_down, rank_up):
    levels = lax.axis_size("feat").bit_length() - 1
    inner = levels - 2
    tok, width = tokens.shape
    rank = rank_down.shape[1]
    own = tok >> inner
    bf16 = jnp.bfloat16
    dma = pltpu.SemaphoreType.DMA
    any_spec = pl.BlockSpec(memory_space=pl.ANY)
    return pl.pallas_call(
        functools.partial(kernel, levels),
        out_shape=jax.ShapeDtypeStruct((tok, width), bf16),
        in_specs=[any_spec] * 4,
        out_specs=any_spec,
        scratch_shapes=[
            pltpu.VMEM((tok, width), bf16),
            pltpu.VMEM(pair_weights.shape[1:], bf16),
            pltpu.VMEM(pair_weights.shape[1:], bf16),
            pltpu.VMEM((width, rank), bf16),
            pltpu.VMEM((rank, width), bf16),
            pltpu.VMEM((tok, width), bf16),
            pltpu.VMEM((tok, width), bf16),
            pltpu.VMEM((tok, width), bf16),
            pltpu.VMEM((tok, width), bf16),
            pltpu.VMEM((tok, rank), jnp.float32),
            pltpu.VMEM((tok, rank), bf16),
            pltpu.VMEM((tok, rank), bf16),
            pltpu.VMEM((tok, rank), bf16),
            pltpu.VMEM((own, rank), bf16),
            pltpu.VMEM((own, rank), bf16),
            pltpu.VMEM((own, rank), bf16),
            pltpu.VMEM((own, rank), bf16),
            dma((5,)), dma((CHUNKS,)),
            dma((CHUNKS,)), dma((CHUNKS,)), dma((CHUNKS,)), dma((CHUNKS,)),
            dma((inner,)), dma((inner,)), dma((inner,)), dma((inner,)),
            dma((1,)), dma((1,)), dma((1,)), dma((1,)), dma((1,)), dma((1,)),
        ],
        compiler_params=pltpu.CompilerParams(
            collective_id=0, has_side_effects=True, vmem_limit_bytes=60 * 2**20
        ),
    )(tokens, pair_weights, rank_down, rank_up)


def solution(mesh):
    return jax.shard_map(
        on_device,
        mesh=mesh,
        in_specs=(P("tok", "feat"), P(None, None, "feat"), P("feat", None), P(None, "feat")),
        out_specs=P("tok", "feat"),
        check_vma=False,
    )
```

```python
import functools

import jax
import jax.numpy as jnp
from jax import lax
from jax.experimental import pallas as pl
from jax.experimental.pallas import tpu as pltpu
from jax.sharding import PartitionSpec as P

CHUNKS = 16
MESH = pl.DeviceIdType.MESH


def silu(v):
    return v / (1.0 + jnp.exp(-v))


def flip(me, bits):
    other = me
    for b in bits:
        other = other + (1 - 2 * ((me // (1 << b)) % 2)) * (1 << b)
    return other


def kernel(
    levels, x_hbm, w_hbm, down_hbm, up_hbm, out_hbm,
    x, w0, w1, down, up, xp, state, sp, out,
    acc, low, send_buf, recv_buf, end_recv, mid_recv, end_send, mid_send,
    load_sem, out_sem, ys, yr, zs, zr, rs_s, rs_r, ag_s, ag_r,
    end_s, end_r, mid_s, mid_r, back_s, back_r,
):
    me = lax.axis_index("feat")
    tok, width = x.shape
    rows = tok // CHUNKS
    top = levels - 1
    inner = top - 1

    loads = [
        pltpu.make_async_copy(src, dst, load_sem.at[i])
        for i, (src, dst) in enumerate(
            ((x_hbm, x), (down_hbm, down), (w_hbm.at[0], w0), (w_hbm.at[1], w1), (up_hbm, up))
        )
    ]
    for load in loads:
        load.start()

    partners = [flip(me, (b,)) for b in range(levels)] + [flip(me, (inner, top))]
    barrier = pltpu.get_barrier_semaphore()
    for other in partners:
        pl.semaphore_signal(barrier, inc=1, device_id={"feat": other}, device_id_type=MESH)
    pl.semaphore_wait(barrier, len(partners))

    def remote(src, dst, send, recv, other):
        return pltpu.make_async_remote_copy(
            src_ref=src, dst_ref=dst, send_sem=send, recv_sem=recv,
            device_id={"feat": other}, device_id_type=MESH,
        )

    def part(c):
        return pl.ds(pl.multiple_of(c * rows, rows), rows)

    def y_copy(c):
        return remote(x_hbm.at[part(c)], xp.at[part(c)], ys.at[c], yr.at[c], partners[0])

    def z_copy(c):
        return remote(state.at[part(c)], sp.at[part(c)], zs.at[c], zr.at[c], partners[top])

    def out_copy(c):
        return pltpu.make_async_copy(out.at[part(c)], out_hbm.at[part(c)], out_sem.at[c])

    y_copy(0).start()

    loads[0].wait()
    loads[1].wait()
    bit = [(me // (1 << b)) % 2 for b in range(levels)]
    step_rows = tok // 8

    def project(offset, count):
        @pl.loop(0, count // step_rows)
        def _(i):
            span = pl.ds(pl.multiple_of(offset + i * step_rows, step_rows), step_rows)
            acc[span, :] = jnp.dot(x[span, :], down[...], preferred_element_type=jnp.float32)

    def span_of(offset, count):
        return pl.ds(pl.multiple_of(offset, count), count)

    half = tok // 2
    keep = bit[0] * half
    away = (1 - bit[0]) * half
    project(away, half)
    spans = [(keep, away, half)]
    for b in range(1, inner):
        size = spans[-1][2] // 2
        base = spans[-1][0]
        spans.append((base + bit[b] * size, base + (1 - bit[b]) * size, size))

    def rs_copy(b):
        size = spans[b][2]
        start = tok - 2 * size
        return remote(
            send_buf.at[pl.ds(start, size)], recv_buf.at[pl.ds(start, size)],
            rs_s.at[b], rs_r.at[b], partners[b],
        )

    def rs_start(b):
        _, gone, size = spans[b]
        send_buf[pl.ds(tok - 2 * size, size), :] = acc[span_of(gone, size), :].astype(jnp.bfloat16)
        rs_copy(b).start()

    def rs_finish(b):
        kept, _, size = spans[b]
        rs_copy(b).wait_recv()
        acc[span_of(kept, size), :] += recv_buf[pl.ds(tok - 2 * size, size), :].astype(jnp.float32)

    rs_start(0)
    for c in range(1, CHUNKS):
        y_copy(c).start()
    project(keep, half)

    own, _, own_size = spans[-1]
    own_span = span_of(own, own_size)
    middle = (bit[inner] + bit[top]) % 2
    end_copy = remote(end_send, end_recv, end_s.at[0], end_r.at[0], partners[inner])
    mid_copy = remote(mid_send, mid_recv, mid_s.at[0], mid_r.at[0], partners[levels])
    back_copy = remote(low.at[own_span], low.at[own_span], back_s.at[0], back_r.at[0], partners[inner])

    def to_middle():
        @pl.when(middle == 0)
        def _():
            end_send[...] = acc[own_span, :].astype(jnp.bfloat16)
            end_copy.start()

    def across():
        @pl.when(middle == 1)
        def _():
            end_copy.wait_recv()
            acc[own_span, :] += end_recv[...].astype(jnp.float32)
            mid_send[...] = acc[own_span, :].astype(jnp.bfloat16)
            mid_copy.start()

    def back():
        @pl.when(middle == 1)
        def _():
            mid_copy.wait_recv()
            low[own_span, :] = (acc[own_span, :] + mid_recv[...].astype(jnp.float32)).astype(jnp.bfloat16)
            back_copy.start()

    def ag_copy(b):
        size = tok >> (b + 1)
        span = span_of(spans[b][0], size)
        return remote(low.at[span], low.at[span], ag_s.at[b], ag_r.at[b], partners[b])

    columns = 512
    column_tiles = width // columns

    def first_section(c):
        y_copy(c).wait_recv()

        @pl.loop(0, column_tiles)
        def _(t):
            cols = pl.ds(pl.multiple_of(t * columns, columns), columns)
            pre = jnp.dot(x[part(c), :], w0[:width, cols], preferred_element_type=jnp.float32)
            pre += jnp.dot(xp[part(c), :], w0[width:, cols], preferred_element_type=jnp.float32)
            state[part(c), cols] = silu(pre).astype(jnp.bfloat16)

        z_copy(c).start()

    def second_section(c):
        z_copy(c).wait_recv()

        @pl.loop(0, column_tiles)
        def _(t):
            cols = pl.ds(pl.multiple_of(t * columns, columns), columns)
            pre = jnp.dot(state[part(c), :], w1[:width, cols], preferred_element_type=jnp.float32)
            pre += jnp.dot(sp[part(c), :], w1[width:, cols], preferred_element_type=jnp.float32)
            side = jnp.dot(low[part(c), :], up[:, cols], preferred_element_type=jnp.float32)
            out[part(c), cols] = (silu(pre) + side).astype(jnp.bfloat16)

        out_copy(c).start()

    def sections(first, last):
        @pl.loop(first, last)
        def _(c):
            first_section(c)

    loads[2].wait()
    sections(0, 1)
    for b in range(inner):
        rs_finish(b)
        if b + 1 < inner:
            rs_start(b + 1)
    to_middle()
    sections(1, 2)
    across()
    hold = 4 + middle * (6 - 4)
    sections(2, hold)
    back()

    @pl.when(middle == 0)
    def _():
        back_copy.wait_recv()

    sections(hold, CHUNKS)

    for b in range(inner - 1, -1, -1):
        ag_copy(b).start()
        ag_copy(b).wait_recv()

    loads[3].wait()
    loads[4].wait()

    @pl.loop(0, CHUNKS)
    def _(c):
        second_section(c)

    @pl.loop(0, CHUNKS)
    def _(c):
        y_copy(c).wait_send()
        z_copy(c).wait_send()
        out_copy(c).wait()

    for b in range(inner):
        rs_copy(b).wait_send()
        ag_copy(b).wait_send()

    @pl.when(middle == 0)
    def _():
        end_copy.wait_send()

    @pl.when(middle == 1)
    def _():
        mid_copy.wait_send()
        back_copy.wait_send()


def on_device(tokens, pair_weights, rank_down, rank_up):
    levels = lax.axis_size("feat").bit_length() - 1
    inner = levels - 2
    tok, width = tokens.shape
    rank = rank_down.shape[1]
    own = tok >> inner
    bf16 = jnp.bfloat16
    dma = pltpu.SemaphoreType.DMA
    any_spec = pl.BlockSpec(memory_space=pl.ANY)
    return pl.pallas_call(
        functools.partial(kernel, levels),
        out_shape=jax.ShapeDtypeStruct((tok, width), bf16),
        in_specs=[any_spec] * 4,
        out_specs=any_spec,
        scratch_shapes=[
            pltpu.VMEM((tok, width), bf16),
            pltpu.VMEM(pair_weights.shape[1:], bf16),
            pltpu.VMEM(pair_weights.shape[1:], bf16),
            pltpu.VMEM((width, rank), bf16),
            pltpu.VMEM((rank, width), bf16),
            pltpu.VMEM((tok, width), bf16),
            pltpu.VMEM((tok, width), bf16),
            pltpu.VMEM((tok, width), bf16),
            pltpu.VMEM((tok, width), bf16),
            pltpu.VMEM((tok, rank), jnp.float32),
            pltpu.VMEM((tok, rank), bf16),
            pltpu.VMEM((tok, rank), bf16),
            pltpu.VMEM((tok, rank), bf16),
            pltpu.VMEM((own, rank), bf16),
            pltpu.VMEM((own, rank), bf16),
            pltpu.VMEM((own, rank), bf16),
            pltpu.VMEM((own, rank), bf16),
            dma((5,)), dma((CHUNKS,)),
            dma((CHUNKS,)), dma((CHUNKS,)), dma((CHUNKS,)), dma((CHUNKS,)),
            dma((inner,)), dma((inner,)), dma((inner,)), dma((inner,)),
            dma((1,)), dma((1,)), dma((1,)), dma((1,)), dma((1,)), dma((1,)),
        ],
        compiler_params=pltpu.CompilerParams(
            collective_id=0, has_side_effects=True, vmem_limit_bytes=60 * 2**20
        ),
    )(tokens, pair_weights, rank_down, rank_up)


def solution(mesh):
    return jax.shard_map(
        on_device,
        mesh=mesh,
        in_specs=(P("tok", "feat"), P(None, None, "feat"), P("feat", None), P(None, "feat")),
        out_specs=P("tok", "feat"),
        check_vma=False,
    )
```

```python
import functools

import jax
import jax.numpy as jnp
from jax import lax
from jax.experimental import pallas as pl
from jax.experimental.pallas import tpu as pltpu
from jax.sharding import PartitionSpec as P

CHUNKS = 16
MESH = pl.DeviceIdType.MESH


def silu(v):
    return v / (1.0 + jnp.exp(-v))


def flip(me, bits):
    other = me
    for b in bits:
        other = other + (1 - 2 * ((me // (1 << b)) % 2)) * (1 << b)
    return other


def kernel(
    levels, x_hbm, w_hbm, down_hbm, up_hbm, out_hbm,
    x, w0, w1, down, up, xp, state, sp, out,
    acc, low, send_buf, recv_buf, end_recv, mid_recv, end_send, mid_send,
    load_sem, out_sem, ys, yr, zs, zr, rs_s, rs_r, ag_s, ag_r,
    end_s, end_r, mid_s, mid_r, back_s, back_r,
):
    me = lax.axis_index("feat")
    tok, width = x.shape
    rows = tok // CHUNKS
    top = levels - 1
    inner = top - 1

    loads = [
        pltpu.make_async_copy(src, dst, load_sem.at[i])
        for i, (src, dst) in enumerate(
            ((x_hbm, x), (down_hbm, down), (w_hbm.at[0], w0), (w_hbm.at[1], w1), (up_hbm, up))
        )
    ]
    for load in loads[:3]:
        load.start()

    partners = [flip(me, (b,)) for b in range(levels)] + [flip(me, (inner, top))]
    barrier = pltpu.get_barrier_semaphore()
    for other in partners:
        pl.semaphore_signal(barrier, inc=1, device_id={"feat": other}, device_id_type=MESH)
    pl.semaphore_wait(barrier, len(partners))

    def remote(src, dst, send, recv, other):
        return pltpu.make_async_remote_copy(
            src_ref=src, dst_ref=dst, send_sem=send, recv_sem=recv,
            device_id={"feat": other}, device_id_type=MESH,
        )

    def part(c):
        return pl.ds(pl.multiple_of(c * rows, rows), rows)

    def y_copy(c):
        return remote(x_hbm.at[part(c)], xp.at[part(c)], ys.at[c], yr.at[c], partners[0])

    def z_copy(c):
        return remote(state.at[part(c)], sp.at[part(c)], zs.at[c], zr.at[c], partners[top])

    def out_copy(c):
        return pltpu.make_async_copy(out.at[part(c)], out_hbm.at[part(c)], out_sem.at[c])

    y_copy(0).start()

    loads[0].wait()
    loads[1].wait()
    bit = [(me // (1 << b)) % 2 for b in range(levels)]
    step_rows = tok // 8

    def project(offset, count):
        @pl.loop(0, count // step_rows)
        def _(i):
            span = pl.ds(pl.multiple_of(offset + i * step_rows, step_rows), step_rows)
            acc[span, :] = jnp.dot(x[span, :], down[...], preferred_element_type=jnp.float32)

    def span_of(offset, count):
        return pl.ds(pl.multiple_of(offset, count), count)

    half = tok // 2
    keep = bit[0] * half
    away = (1 - bit[0]) * half
    project(away, half)
    spans = [(keep, away, half)]
    for b in range(1, inner):
        size = spans[-1][2] // 2
        base = spans[-1][0]
        spans.append((base + bit[b] * size, base + (1 - bit[b]) * size, size))

    def rs_copy(b):
        size = spans[b][2]
        start = tok - 2 * size
        return remote(
            send_buf.at[pl.ds(start, size)], recv_buf.at[pl.ds(start, size)],
            rs_s.at[b], rs_r.at[b], partners[b],
        )

    def rs_start(b):
        _, gone, size = spans[b]
        send_buf[pl.ds(tok - 2 * size, size), :] = acc[span_of(gone, size), :].astype(jnp.bfloat16)
        rs_copy(b).start()

    def rs_finish(b):
        kept, _, size = spans[b]
        rs_copy(b).wait_recv()
        acc[span_of(kept, size), :] += recv_buf[pl.ds(tok - 2 * size, size), :].astype(jnp.float32)

    rs_start(0)
    for c in range(1, CHUNKS):
        y_copy(c).start()
    for load in loads[3:]:
        load.start()

    own, _, own_size = spans[-1]
    own_span = span_of(own, own_size)
    middle = (bit[inner] + bit[top]) % 2
    end_copy = remote(end_send, end_recv, end_s.at[0], end_r.at[0], partners[inner])
    mid_copy = remote(mid_send, mid_recv, mid_s.at[0], mid_r.at[0], partners[levels])
    back_copy = remote(low.at[own_span], low.at[own_span], back_s.at[0], back_r.at[0], partners[inner])

    def to_middle():
        @pl.when(middle == 0)
        def _():
            end_send[...] = acc[own_span, :].astype(jnp.bfloat16)
            end_copy.start()

    def across():
        @pl.when(middle == 1)
        def _():
            end_copy.wait_recv()
            acc[own_span, :] += end_recv[...].astype(jnp.float32)
            mid_send[...] = acc[own_span, :].astype(jnp.bfloat16)
            mid_copy.start()

    def back():
        @pl.when(middle == 1)
        def _():
            mid_copy.wait_recv()
            low[own_span, :] = (acc[own_span, :] + mid_recv[...].astype(jnp.float32)).astype(jnp.bfloat16)
            back_copy.start()

    def ag_copy(b):
        size = tok >> (b + 1)
        span = span_of(spans[b][0], size)
        return remote(low.at[span], low.at[span], ag_s.at[b], ag_r.at[b], partners[b])

    columns = width
    column_tiles = width // columns

    def first_section(c):
        y_copy(c).wait_recv()

        @pl.loop(0, column_tiles)
        def _(t):
            cols = pl.ds(pl.multiple_of(t * columns, columns), columns)
            pre = jnp.dot(x[part(c), :], w0[:width, cols], preferred_element_type=jnp.float32)
            pre += jnp.dot(xp[part(c), :], w0[width:, cols], preferred_element_type=jnp.float32)
            state[part(c), cols] = silu(pre).astype(jnp.bfloat16)

        z_copy(c).start()

    def second_section(c):
        z_copy(c).wait_recv()

        @pl.loop(0, column_tiles)
        def _(t):
            cols = pl.ds(pl.multiple_of(t * columns, columns), columns)
            pre = jnp.dot(state[part(c), :], w1[:width, cols], preferred_element_type=jnp.float32)
            pre += jnp.dot(sp[part(c), :], w1[width:, cols], preferred_element_type=jnp.float32)
            side = jnp.dot(low[part(c), :], up[:, cols], preferred_element_type=jnp.float32)
            out[part(c), cols] = (silu(pre) + side).astype(jnp.bfloat16)

        out_copy(c).start()

    def sections(first, last):
        @pl.loop(first, last)
        def _(c):
            first_section(c)

    loads[2].wait()
    sections(0, 1)
    project(keep, half)
    for b in range(inner):
        rs_finish(b)
        if b + 1 < inner:
            rs_start(b + 1)
    to_middle()
    sections(1, 2)
    across()
    hold = 4 + middle * (6 - 4)
    sections(2, hold)
    back()

    @pl.when(middle == 0)
    def _():
        back_copy.wait_recv()

    sections(hold, CHUNKS)

    for b in range(inner - 1, -1, -1):
        ag_copy(b).start()
        ag_copy(b).wait_recv()

    loads[3].wait()
    loads[4].wait()

    @pl.loop(0, CHUNKS)
    def _(c):
        second_section(c)

    @pl.loop(0, CHUNKS)
    def _(c):
        y_copy(c).wait_send()
        z_copy(c).wait_send()
        out_copy(c).wait()

    for b in range(inner):
        rs_copy(b).wait_send()
        ag_copy(b).wait_send()

    @pl.when(middle == 0)
    def _():
        end_copy.wait_send()

    @pl.when(middle == 1)
    def _():
        mid_copy.wait_send()
        back_copy.wait_send()


def on_device(tokens, pair_weights, rank_down, rank_up):
    levels = lax.axis_size("feat").bit_length() - 1
    inner = levels - 2
    tok, width = tokens.shape
    rank = rank_down.shape[1]
    own = tok >> inner
    bf16 = jnp.bfloat16
    dma = pltpu.SemaphoreType.DMA
    any_spec = pl.BlockSpec(memory_space=pl.ANY)
    return pl.pallas_call(
        functools.partial(kernel, levels),
        out_shape=jax.ShapeDtypeStruct((tok, width), bf16),
        in_specs=[any_spec] * 4,
        out_specs=any_spec,
        scratch_shapes=[
            pltpu.VMEM((tok, width), bf16),
            pltpu.VMEM(pair_weights.shape[1:], bf16),
            pltpu.VMEM(pair_weights.shape[1:], bf16),
            pltpu.VMEM((width, rank), bf16),
            pltpu.VMEM((rank, width), bf16),
            pltpu.VMEM((tok, width), bf16),
            pltpu.VMEM((tok, width), bf16),
            pltpu.VMEM((tok, width), bf16),
            pltpu.VMEM((tok, width), bf16),
            pltpu.VMEM((tok, rank), jnp.float32),
            pltpu.VMEM((tok, rank), bf16),
            pltpu.VMEM((tok, rank), bf16),
            pltpu.VMEM((tok, rank), bf16),
            pltpu.VMEM((own, rank), bf16),
            pltpu.VMEM((own, rank), bf16),
            pltpu.VMEM((own, rank), bf16),
            pltpu.VMEM((own, rank), bf16),
            dma((5,)), dma((CHUNKS,)),
            dma((CHUNKS,)), dma((CHUNKS,)), dma((CHUNKS,)), dma((CHUNKS,)),
            dma((inner,)), dma((inner,)), dma((inner,)), dma((inner,)),
            dma((1,)), dma((1,)), dma((1,)), dma((1,)), dma((1,)), dma((1,)),
        ],
        compiler_params=pltpu.CompilerParams(
            collective_id=0, has_side_effects=True, vmem_limit_bytes=60 * 2**20
        ),
    )(tokens, pair_weights, rank_down, rank_up)


def solution(mesh):
    return jax.shard_map(
        on_device,
        mesh=mesh,
        in_specs=(P("tok", "feat"), P(None, None, "feat"), P("feat", None), P(None, "feat")),
        out_specs=P("tok", "feat"),
        check_vma=False,
    )
```
